32 devices in a mesh: gen: 4 (over x, core), join: 8 (over z, y).
Axes of the slice: x: 2, y: 2, z: 4, core: 2. Of those that a mesh axis runs over, the one named last changes fastest.
Arguments:
- src_emb: bfloat16 [65536, 512], P(('gen', 'join')), may hold values from -64 to 64
- counts: int32 [32, 32], P(('gen', 'join')), may hold values from 0 to 64, as said below
Outputs:
- dup_weight: float32 [65536], P(('gen', 'join'))
The draws below stay inside these ranges and needn't reach their ends.
Inputs may be any that keep to these rules, and one draw needn't show every extreme that they name: Slot c of source s for owner o is live when c < counts[s, o]; in every draw some owner receives 64 live slots from every source.
All inputs are finite; a program needn't handle non-finite values.
Results may differ from the reference program's by a relative error of at most 0.0016.
Values may be sent and summed in bfloat16 or wider, within the bound.
A program may use at most 64 MiB of HBM per device.

```python
import math
import jax
import jax.numpy as jnp
from jax import lax

D = 512
BLOCK = 2048
ROUNDS = 3
NODES = 32
CAP = 64
ROWS = 65536
N_GEN = 4
N_JOIN = 8


def draw_src_emb(key, part):
    keys = jax.random.split(key, 4)
    clusters = max(ROWS // 16, 1)
    centers = jnp.clip(jax.random.normal(keys[0], (clusters, D), jnp.float32), -4.0, 4.0)
    members = jax.random.randint(keys[1], (ROWS,), 0, clusters)
    noise = 0.4 * jnp.clip(jax.random.normal(keys[2], (ROWS, D), jnp.float32), -6.0, 6.0)
    scale = jnp.exp(jax.random.uniform(keys[3], (ROWS, 1), jnp.float32, math.log(0.5), math.log(5.0)))
    values = (centers[members] + noise) * scale
    return values.astype(jnp.bfloat16)


def draw_counts(key, part):
    keys = jax.random.split(key, 5)
    lowest = max(1, CAP * 5 // 8)
    limits = jax.random.randint(keys[0], (NODES,), lowest, CAP + 1)
    raw = jax.random.randint(keys[1], (NODES, NODES), 0, 1048576)
    drawn = limits[None, :] - raw % (limits[None, :] // 2 + 1)
    full_owner = jax.random.randint(keys[2], (), 0, NODES)
    empty_source = jax.random.randint(keys[3], (), 0, NODES)
    empty_owner = (full_owner + 1 + jax.random.randint(keys[4], (), 0, NODES - 1)) % NODES
    column = lax.broadcasted_iota(jnp.int32, (NODES, NODES), 1)
    row = lax.broadcasted_iota(jnp.int32, (NODES, NODES), 0)
    result = jnp.where(column == full_owner, CAP, drawn)
    result = jnp.where((row == empty_source) & (column == empty_owner), 0, result)
    return result.astype(jnp.int32)


def setup_inputs(seed: int = 0) -> dict:
    key_of = jax.random.split(jax.random.key(seed), 3)
    return {
        "src_emb": draw_src_emb(jax.random.fold_in(key_of[2], 71), 0),
        "counts": draw_counts(jax.random.fold_in(key_of[2], 71), 0),
    }


def normalize(src_emb):
    values = src_emb.astype(jnp.float32)
    scaled = values * lax.rsqrt(lax.optimization_barrier(jnp.mean(values * values, axis=1, keepdims=True)) + 1e-06) / math.sqrt(D)
    return scaled.astype(jnp.bfloat16)

def tile_sums(left_rows, left_live, right_rows, right_live):
    scores = jnp.dot(left_rows, right_rows.T, preferred_element_type=jnp.float32)
    kernel = jnp.exp(8.0 * (scores - 1.0))
    return (lax.optimization_barrier(jnp.sum(kernel * right_live[None, :], axis=1)), lax.optimization_barrier(jnp.sum(kernel * left_live[:, None], axis=0)))

def own_tile(operands):
    return tile_sums(operands[0], operands[1], operands[0], operands[1])[0]

def cross_tile(operands):
    return tile_sums(operands[0], operands[1], operands[2], operands[3])

def flatten(array):
    return array.reshape((NODES,) + array.shape[2:])

def reference(src_emb, counts):
    unit = normalize(src_emb)
    blocks = unit.reshape(NODES, NODES, CAP, D).transpose(1, 0, 2, 3).reshape(N_GEN, N_JOIN, BLOCK, D)
    slot_index = jnp.arange(CAP).astype(jnp.int32)
    live = (slot_index[None, None, :] < counts[:, :, None]).astype(jnp.float32)
    live = live.transpose(1, 0, 2).reshape(N_GEN, N_JOIN, BLOCK)
    density = lax.map(own_tile, (flatten(blocks), flatten(live))).reshape(N_GEN, N_JOIN, BLOCK)
    for offset in range(1, ROUNDS + 1):
        moved_blocks = jnp.roll(blocks, offset, axis=1)
        moved_live = jnp.roll(live, offset, axis=1)
        row_sums, col_sums = lax.map(cross_tile, (flatten(blocks), flatten(live), flatten(moved_blocks), flatten(moved_live)))
        density = density + row_sums.reshape(N_GEN, N_JOIN, BLOCK)
        density = density + jnp.roll(col_sums.reshape(N_GEN, N_JOIN, BLOCK), -offset, axis=1)
    weight = live / (density + 1.0 - live)
    return weight.reshape(ROWS)
```

```python
import math

import jax
import jax.numpy as jnp
from jax import lax
from jax.experimental import pallas as pl
from jax.experimental.pallas import tpu as pltpu
from jax.sharding import PartitionSpec as P

ROUNDS = 3
MESH = pl.DeviceIdType.MESH
SCALE = 8.0 * math.log2(math.e)
DEAD = -1e30
LAYERS = 4
OWN, YN, SIB, XN, XS = range(5)


def shifted(block, axis, distance):
    devices = range(lax.axis_size(axis))
    route = [((i - distance) % len(devices), i) for i in devices]
    return lax.ppermute(block, axis, route)


def tile_sums(left_rows, left_live, right_rows, right_live):
    row_count = left_rows.shape[0]
    piece_rows = min(512, row_count)
    pieces = row_count // piece_rows

    def one_piece(col_total, operands):
        piece_block, piece_live = operands
        scores = lax.dot_general(
            piece_block, right_rows, (((1,), (1,)), ((), ())), preferred_element_type=jnp.float32
        )
        kernel = jnp.exp(8.0 * (scores - 1.0))
        return (
            col_total + jnp.sum(kernel * piece_live[:, None], axis=0),
            jnp.sum(kernel * right_live[None, :], axis=1),
        )

    start_total = jnp.zeros((right_rows.shape[0],), jnp.float32)
    col_sums, row_sums = lax.scan(
        one_piece,
        start_total,
        (
            left_rows.reshape(pieces, piece_rows, left_rows.shape[1]),
            left_live.reshape(pieces, piece_rows),
        ),
    )
    return (row_sums.reshape(row_count), col_sums)


def ring_body(src_emb, counts):
    values = src_emb.astype(jnp.float32)
    width = values.shape[1]
    unit = (
        values
        * lax.rsqrt(jnp.mean(values * values, axis=1, keepdims=True) + 1e-06)
        / math.sqrt(width)
    ).astype(jnp.bfloat16)
    nodes = lax.axis_size(("gen", "join"))
    block_rows = unit.shape[0]
    slots = block_rows // nodes
    received, got_counts = (
        lax.all_to_all(
            unit.reshape(nodes, slots, width),
            ("gen", "join"),
            split_axis=0,
            concat_axis=0,
            tiled=True,
        ),
        lax.all_to_all(
            counts.reshape(nodes), ("gen", "join"), split_axis=0, concat_axis=0, tiled=True
        ),
    )
    owned = received.reshape(block_rows, width)
    slot_index = lax.broadcasted_iota(jnp.int32, (nodes, slots), 1)
    live = (slot_index < got_counts.reshape(nodes, 1)).astype(jnp.float32).reshape(block_rows)
    live_wire = live.astype(jnp.bfloat16)
    density = tile_sums(owned, live, owned, live)[0]
    for shift_by in range(1, ROUNDS + 1):
        other_rows, other_flags = shifted((owned, live_wire), "join", shift_by)
        row_sums, col_sums = tile_sums(owned, live, other_rows, other_flags.astype(jnp.float32))
        density = density + row_sums + shifted(col_sums, "join", -shift_by)
    return live / (density + 1.0 - live)


def layer_kernel(rows, width, src, flags, out, buf, snd, bias, acc, part, got, ws, wr,
                 zsend, zrecv, lsend, lrecv, psem, wsend, wrecv):
    gen, join = lax.axis_index("gen"), lax.axis_index("join")
    x, k, z, y = gen // 2, gen % 2, join // 2, join % 2
    zh, zl = z // 2, z % 2
    layer = [z, 2 * zh + 1 - zl, 2 * (1 - zh) + zl, 3 - z]
    nodes, joins = 32, 8
    me = gen * joins + join
    sibling = (2 * x + 1 - k, join)
    x_near = (2 * (1 - x) + k, join)
    y_near = (gen, 2 * z + 1 - y)
    owners = 8
    slots = rows // owners

    barrier = pltpu.get_barrier_semaphore()

    def greet(i, carry):
        t = (me + i) % nodes
        pl.semaphore_signal(barrier, inc=1, device_id=(t // joins, t % joins), device_id_type=MESH)
        return carry

    lax.fori_loop(1, nodes, greet, 0)

    def normalize(d, into):
        start = pl.multiple_of(layer[d] * rows, rows)
        values = src[pl.ds(start, rows), :].astype(jnp.float32)
        into[0:rows, :] = (
            values
            * lax.rsqrt(jnp.mean(values * values, axis=1, keepdims=True) + 1e-06)
            / math.sqrt(width)
        ).astype(jnp.bfloat16)
        into[rows:rows + 16, :] = flags[layer[d]]

    def z_copy(d):
        return pltpu.make_async_remote_copy(
            src_ref=snd.at[d - 1], dst_ref=buf.at[5 * d + OWN], send_sem=zsend.at[d - 1],
            recv_sem=zrecv.at[d - 1], device_id=(gen, 2 * layer[d] + y), device_id_type=MESH,
        )

    def l_copy(d, kind):
        source = XN if kind == XS else OWN
        target = {SIB: sibling, XS: sibling, XN: x_near, YN: y_near}[kind]
        return pltpu.make_async_remote_copy(
            src_ref=buf.at[5 * d + source], dst_ref=buf.at[5 * d + kind],
            send_sem=lsend.at[4 * d + kind - 1], recv_sem=lrecv.at[4 * d + kind - 1],
            device_id=target, device_id_type=MESH,
        )

    def set_bias(d, kind):
        slot = 4 * d + max(kind - 1, 0)
        ones = jnp.full((16, 128), 1.0 / 16.0, jnp.bfloat16)
        live = lax.dot_general(
            buf[5 * d + kind, rows:rows + 16, :], ones, (((0,), (0,)), ((), ())),
            preferred_element_type=jnp.float32,
        )
        bias[slot] = jnp.where(live > 0.5, -SCALE, DEAD)

    piece = 128

    def tile(row, row_slot, col, col_slot):
        held = buf[row, 0:rows, :]
        for b in range(rows // piece):
            scores = lax.dot_general(
                buf[col, b * piece:(b + 1) * piece, :], held, (((1,), (1,)), ((), ())),
                preferred_element_type=jnp.float32,
            )
            shift = bias[col_slot, b * piece:(b + 1) * piece, :]
            kernel = jnp.exp2(scores * SCALE + jnp.concatenate([shift] * (rows // 128), axis=1))
            count = piece // slots
            sums = jnp.sum(kernel.reshape(count, slots // 8, 8, rows), axis=1)
            acc[row_slot, 8 * count * b:8 * count * (b + 1), :] += sums.reshape(8 * count, rows)

    def over_rows(count, col, col_slot):
        def step(i, carry):
            tile(5 * (i // 2) + i % 2, i, col, col_slot)
            return carry

        lax.fori_loop(0, count, step, 0)

    def over_cols(count, row, row_slot):
        def step(i, carry):
            c, kk = i // 4, i % 4
            tile(row, row_slot, 5 * c + kk + (kk + 3) // 4, i)
            return carry

        lax.fori_loop(0, count, step, 0)

    normalize(2, snd.at[1])
    normalize(0, buf.at[OWN])
    pl.semaphore_wait(barrier, nodes - 1)
    z_copy(2).start()
    l_copy(0, XN).start()
    l_copy(0, YN).start()
    l_copy(0, SIB).start()
    normalize(1, snd.at[0])
    z_copy(1).start()
    normalize(3, snd.at[2])
    z_copy(3).start()
    acc[...] = jnp.zeros_like(acc)
    part[...] = jnp.zeros_like(part)
    ws[...] = jnp.zeros_like(ws)

    def z_wait(d):
        pltpu.make_async_remote_copy(
            src_ref=snd.at[d - 1], dst_ref=buf.at[5 * d + OWN], send_sem=zsend.at[d - 1],
            recv_sem=zrecv.at[d - 1], device_id=y_near, device_id_type=MESH,
        ).wait_recv()

    def phase(d, carry):
        @pl.when(d > 0)
        def _():
            z_wait(d)
            l_copy(d, XN).start()
            l_copy(d, YN).start()
            l_copy(d, SIB).start()

        set_bias(d, OWN)
        over_cols(4 * d, 5 * d + OWN, 2 * d)
        over_rows(2 * d + 1, 5 * d + OWN, 4 * d)
        l_copy(d, SIB).wait_recv()
        set_bias(d, SIB)
        over_rows(2 * d + 1, 5 * d + SIB, 4 * d + 1)
        l_copy(d, XN).wait_recv()
        l_copy(d, XS).start()
        set_bias(d, XN)
        over_rows(2 * d + 1, 5 * d + XN, 4 * d + 2)
        l_copy(d, YN).wait_recv()
        over_cols(4 * d + 3, 5 * d + YN, 2 * d + 1)
        l_copy(d, XS).wait_recv()
        set_bias(d, XS)
        over_rows(2 * d + 2, 5 * d + XS, 4 * d + 3)
        return carry

    lax.fori_loop(0, LAYERS, phase, 0)

    col_owner = lax.broadcasted_iota(jnp.int32, (8 * owners, rows), 0) // 8
    row_owner = lax.broadcasted_iota(jnp.int32, (8 * owners, rows), 1) // slots
    near = ((col_owner + 4) % owners != row_owner).astype(jnp.float32)

    def total(i):
        return jnp.sum(acc[i] * near, axis=0, keepdims=True)

    for d in range(LAYERS):
        part[d:d + 1, :] = total(2 * d + 1)
    p_copy = pltpu.make_async_remote_copy(
        src_ref=part, dst_ref=got, send_sem=psem.at[0], recv_sem=psem.at[1],
        device_id=y_near, device_id_type=MESH,
    )
    p_copy.start()
    mine = [total(2 * d) for d in range(LAYERS)]
    p_copy.wait()
    for d in range(LAYERS):
        live = buf[5 * d + OWN, rows:rows + 16, :].astype(jnp.float32)[0:1, :]
        weight = live / (mine[d] + got[d:d + 1, :] + 1.0 - live)
        for j in range(owners):
            ws[j, pl.ds(layer[d], 1), 0:slots] = weight[:, j * slots:(j + 1) * slots]

    spot = 2 * gen + y

    def w_copy(j):
        return pltpu.make_async_remote_copy(
            src_ref=ws.at[j], dst_ref=wr.at[spot], send_sem=wsend.at[j],
            recv_sem=wrecv.at[spot], device_id=(z, j), device_id_type=MESH,
        )

    def w_got(i):
        return pltpu.make_async_remote_copy(
            src_ref=ws.at[0], dst_ref=wr.at[i], send_sem=wsend.at[0],
            recv_sem=wrecv.at[i], device_id=y_near, device_id_type=MESH,
        )

    def send(j, carry):
        @pl.when(z * joins + j != me)
        def _():
            w_copy(j).start()

        @pl.when(z * joins + j == me)
        def _():
            wr[spot] = ws[j]

        return carry

    lax.fori_loop(0, owners, send, 0)

    def receive(i, carry):
        @pl.when((i // 2) * joins + 2 * gen + i % 2 != me)
        def _():
            w_got(i).wait_recv()

        return carry

    lax.fori_loop(0, owners, receive, 0)
    out[...] = wr[...]

    def sent(j, carry):
        @pl.when(z * joins + j != me)
        def _():
            w_copy(j).wait_send()

        return carry

    lax.fori_loop(0, owners, sent, 0)
    for d in range(1, LAYERS):
        z_copy(d).wait_send()
    for d in range(LAYERS):
        for kind in (SIB, XN, YN, XS):
            l_copy(d, kind).wait_send()


def layer_body(src_emb, counts):
    block, width = src_emb.shape
    rows = block // LAYERS
    owners = 8
    slots = rows // owners
    slot = lax.broadcasted_iota(jnp.int32, (LAYERS, 16, owners, slots), 3)
    flags = (slot < counts.reshape(LAYERS, 1, owners, 1)).astype(jnp.bfloat16)
    flags = flags.reshape(LAYERS, 16, rows)
    vmem = pl.BlockSpec(memory_space=pltpu.VMEM)
    weights = pl.pallas_call(
        lambda *refs: layer_kernel(rows, width, *refs),
        out_shape=jax.ShapeDtypeStruct((owners, 8, 128), jnp.float32),
        in_specs=[vmem, vmem],
        out_specs=vmem,
        scratch_shapes=[
            pltpu.VMEM((5 * LAYERS, rows + 16, width), jnp.bfloat16),
            pltpu.VMEM((LAYERS - 1, rows + 16, width), jnp.bfloat16),
            pltpu.VMEM((4 * LAYERS, rows, 128), jnp.float32),
            pltpu.VMEM((2 * LAYERS, 8 * owners, rows), jnp.float32),
            pltpu.VMEM((8, rows), jnp.float32),
            pltpu.VMEM((8, rows), jnp.float32),
            pltpu.VMEM((owners, 8, 128), jnp.float32),
            pltpu.VMEM((owners, 8, 128), jnp.float32),
            pltpu.SemaphoreType.DMA((LAYERS - 1,)),
            pltpu.SemaphoreType.DMA((LAYERS - 1,)),
            pltpu.SemaphoreType.DMA((4 * LAYERS,)),
            pltpu.SemaphoreType.DMA((4 * LAYERS,)),
            pltpu.SemaphoreType.DMA((2,)),
            pltpu.SemaphoreType.DMA((owners,)),
            pltpu.SemaphoreType.DMA((owners,)),
        ],
        compiler_params=pltpu.CompilerParams(
            collective_id=0, has_side_effects=True, vmem_limit_bytes=56 * 2**20
        ),
        name="layer_kernel",
    )(src_emb, flags)
    weights = weights[:, :LAYERS, :slots].reshape(4, 2, LAYERS, slots)
    return weights.transpose(0, 2, 1, 3).reshape(block)


def solution(mesh):
    in_specs = (P(("gen", "join"), None), P(("gen", "join"), None))
    out_specs = P(("gen", "join"))
    fits = mesh.shape["gen"] == 4 and mesh.shape["join"] == 8
    body = layer_body if fits else ring_body
    return jax.shard_map(body, mesh=mesh, in_specs=in_specs, out_specs=out_specs, check_vma=False)
```

```python
import math

import jax
import jax.numpy as jnp
from jax import lax
from jax.experimental import pallas as pl
from jax.experimental.pallas import tpu as pltpu
from jax.sharding import PartitionSpec as P

ROUNDS = 3
MESH = pl.DeviceIdType.MESH
SCALE = 8.0 * math.log2(math.e)
DEAD = -1e30
LAYERS = 4
OWN, YN, SIB, XN, XS = range(5)


def shifted(block, axis, distance):
    devices = range(lax.axis_size(axis))
    route = [((i - distance) % len(devices), i) for i in devices]
    return lax.ppermute(block, axis, route)


def tile_sums(left_rows, left_live, right_rows, right_live):
    row_count = left_rows.shape[0]
    piece_rows = min(512, row_count)
    pieces = row_count // piece_rows

    def one_piece(col_total, operands):
        piece_block, piece_live = operands
        scores = lax.dot_general(
            piece_block, right_rows, (((1,), (1,)), ((), ())), preferred_element_type=jnp.float32
        )
        kernel = jnp.exp(8.0 * (scores - 1.0))
        return (
            col_total + jnp.sum(kernel * piece_live[:, None], axis=0),
            jnp.sum(kernel * right_live[None, :], axis=1),
        )

    start_total = jnp.zeros((right_rows.shape[0],), jnp.float32)
    col_sums, row_sums = lax.scan(
        one_piece,
        start_total,
        (
            left_rows.reshape(pieces, piece_rows, left_rows.shape[1]),
            left_live.reshape(pieces, piece_rows),
        ),
    )
    return (row_sums.reshape(row_count), col_sums)


def ring_body(src_emb, counts):
    values = src_emb.astype(jnp.float32)
    width = values.shape[1]
    unit = (
        values
        * lax.rsqrt(jnp.mean(values * values, axis=1, keepdims=True) + 1e-06)
        / math.sqrt(width)
    ).astype(jnp.bfloat16)
    nodes = lax.axis_size(("gen", "join"))
    block_rows = unit.shape[0]
    slots = block_rows // nodes
    received, got_counts = (
        lax.all_to_all(
            unit.reshape(nodes, slots, width),
            ("gen", "join"),
            split_axis=0,
            concat_axis=0,
            tiled=True,
        ),
        lax.all_to_all(
            counts.reshape(nodes), ("gen", "join"), split_axis=0, concat_axis=0, tiled=True
        ),
    )
    owned = received.reshape(block_rows, width)
    slot_index = lax.broadcasted_iota(jnp.int32, (nodes, slots), 1)
    live = (slot_index < got_counts.reshape(nodes, 1)).astype(jnp.float32).reshape(block_rows)
    live_wire = live.astype(jnp.bfloat16)
    density = tile_sums(owned, live, owned, live)[0]
    for shift_by in range(1, ROUNDS + 1):
        other_rows, other_flags = shifted((owned, live_wire), "join", shift_by)
        row_sums, col_sums = tile_sums(owned, live, other_rows, other_flags.astype(jnp.float32))
        density = density + row_sums + shifted(col_sums, "join", -shift_by)
    return live / (density + 1.0 - live)


def layer_kernel(rows, width, src, flags, out, buf, snd, bias, mask, acc, cacc, ps, got, ws, wr,
                 zsend, zrecv, lsend, lrecv, psem, wsend, wrecv):
    gen, join = lax.axis_index("gen"), lax.axis_index("join")
    x, k, z, y = gen // 2, gen % 2, join // 2, join % 2
    zh, zl = z // 2, z % 2
    layer = [z, 2 * zh + 1 - zl, 2 * (1 - zh) + zl, 3 - z]
    nodes, joins = 32, 8
    me = gen * joins + join
    sibling = (2 * x + 1 - k, join)
    x_near = (2 * (1 - x) + k, join)
    y_near = (gen, 2 * z + 1 - y)
    owners = 8
    slots = rows // owners

    barrier = pltpu.get_barrier_semaphore()

    def greet(i, carry):
        t = (me + i) % nodes
        pl.semaphore_signal(barrier, inc=1, device_id=(t // joins, t % joins), device_id_type=MESH)
        return carry

    lax.fori_loop(1, nodes, greet, 0)

    def normalize(d, into):
        start = pl.multiple_of(layer[d] * rows, rows)
        values = src[pl.ds(start, rows), :].astype(jnp.float32)
        into[0:rows, :] = (
            values
            * lax.rsqrt(jnp.mean(values * values, axis=1, keepdims=True) + 1e-06)
            / math.sqrt(width)
        ).astype(jnp.bfloat16)
        into[rows:rows + 16, :] = flags[layer[d]]

    def z_copy(d):
        return pltpu.make_async_remote_copy(
            src_ref=snd.at[d - 1], dst_ref=buf.at[5 * d + OWN], send_sem=zsend.at[d - 1],
            recv_sem=zrecv.at[d - 1], device_id=(gen, 2 * layer[d] + y), device_id_type=MESH,
        )

    def l_copy(d, kind):
        source = XN if kind == XS else OWN
        target = {SIB: sibling, XS: sibling, XN: x_near, YN: y_near}[kind]
        return pltpu.make_async_remote_copy(
            src_ref=buf.at[5 * d + source], dst_ref=buf.at[5 * d + kind],
            send_sem=lsend.at[4 * d + kind - 1], recv_sem=lrecv.at[4 * d + kind - 1],
            device_id=target, device_id_type=MESH,
        )

    lane_owner = lax.broadcasted_iota(jnp.int32, (owners, rows), 1) // slots
    other_owner = (lax.broadcasted_iota(jnp.int32, (owners, rows), 0) + 4) % owners
    near = (other_owner != lane_owner).astype(jnp.float32)

    def at(kind):
        return max(kind - 1, 0)

    def set_bias(d, kind):
        ones = jnp.full((16, 128), 1.0 / 16.0, jnp.bfloat16)
        live = lax.dot_general(
            buf[5 * d + kind, rows:rows + 16, :], ones, (((0,), (0,)), ((), ())),
            preferred_element_type=jnp.float32,
        )
        bias[at(kind)] = jnp.where(live > 0.5, -SCALE, DEAD)

    def set_mask(d, kind):
        live = buf[5 * d + kind, rows:rows + 16, :].astype(jnp.float32)[0:owners, :]
        mask[2 * d + kind] = live * near

    piece = 256

    def tile(row, slot, col, col_slot, both):
        held = buf[row, 0:rows, :]
        for b in range(rows // piece):
            scores = lax.dot_general(
                buf[col, b * piece:(b + 1) * piece, :], held, (((1,), (1,)), ((), ())),
                preferred_element_type=jnp.float32,
            )
            shift = bias[col_slot, b * piece:(b + 1) * piece, :]
            kernel = jnp.exp2(scores * SCALE + jnp.concatenate([shift] * (rows // 128), axis=1))
            count = piece // slots
            kept = mask[slot, count * b:count * (b + 1), :]
            kernel = (kernel.reshape(count, slots, rows) * kept[:, None, :]).reshape(piece, rows)
            acc[slot] += jnp.sum(kernel.reshape(piece // 8, 8, rows), axis=0)
            if both:
                sums = kernel[:, 0:128]
                for t in range(1, rows // 128):
                    sums = sums + kernel[:, 128 * t:128 * (t + 1)]
                cacc[col_slot, b * piece:(b + 1) * piece, :] += sums

    def old_rows(d, kind):
        def step(i, carry):
            tile(5 * (i // 2) + i % 2, i, 5 * d + kind, at(kind), True)
            return carry

        lax.fori_loop(0, 2 * d, step, 0)

    normalize(2, snd.at[1])
    normalize(0, buf.at[OWN])
    pl.semaphore_wait(barrier, nodes - 1)
    z_copy(2).start()
    l_copy(0, XN).start()
    l_copy(0, YN).start()
    l_copy(0, SIB).start()
    normalize(1, snd.at[0])
    z_copy(1).start()
    normalize(3, snd.at[2])
    z_copy(3).start()
    acc[...] = jnp.zeros_like(acc)
    ps[...] = jnp.zeros_like(ps)
    ws[...] = jnp.zeros_like(ws)

    def z_wait(d):
        pltpu.make_async_remote_copy(
            src_ref=snd.at[d - 1], dst_ref=buf.at[5 * d + OWN], send_sem=zsend.at[d - 1],
            recv_sem=zrecv.at[d - 1], device_id=y_near, device_id_type=MESH,
        ).wait_recv()

    def phase(d, carry):
        cacc[...] = jnp.zeros_like(cacc)
        set_bias(d, OWN)
        set_mask(d, OWN)
        tile(5 * d + OWN, 2 * d, 5 * d + OWN, at(OWN), False)
        old_rows(d, OWN)
        l_copy(d, SIB).wait_recv()
        set_bias(d, SIB)
        tile(5 * d + OWN, 2 * d, 5 * d + SIB, at(SIB), False)
        old_rows(d, SIB)
        l_copy(d, XN).wait_recv()
        l_copy(d, XS).start()

        @pl.when(d < LAYERS - 1)
        def _():
            z_wait(d + 1)
            l_copy(d + 1, XN).start()
            l_copy(d + 1, YN).start()
            l_copy(d + 1, SIB).start()

        set_bias(d, XN)
        tile(5 * d + OWN, 2 * d, 5 * d + XN, at(XN), False)
        old_rows(d, XN)
        l_copy(d, YN).wait_recv()
        set_mask(d, YN)

        def new_row(kk, inner):
            tile(5 * d + YN, 2 * d + 1, 5 * d + kk + (kk + 3) // 4, kk, False)
            return inner

        lax.fori_loop(0, 3, new_row, 0)
        l_copy(d, XS).wait_recv()
        set_bias(d, XS)
        old_rows(d, XS)

        def both_rows(kind, inner):
            tile(5 * d + kind, 2 * d + kind, 5 * d + XS, at(XS), False)
            return inner

        lax.fori_loop(0, 2, both_rows, 0)
        ones = jnp.ones((8, 128), jnp.float32)
        for slot in range(4):
            sums = lax.dot_general(
                ones, cacc[slot], (((1,), (1,)), ((), ())),
                preferred_element_type=jnp.float32, precision=lax.Precision.HIGHEST,
            )
            ps[slot, pl.ds(d, 1), :] = sums[0:1, :]
        return carry

    lax.fori_loop(0, LAYERS, phase, 0)

    def total(i):
        return jnp.sum(acc[i], axis=0, keepdims=True)

    for d in range(LAYERS):
        ps[4, d:d + 1, :] = total(2 * d + 1)
    x_sibling = (2 * (1 - x) + 1 - k, join)
    p_copies = [
        pltpu.make_async_remote_copy(
            src_ref=ps.at[i], dst_ref=got.at[i - 1], send_sem=psem.at[i - 1],
            recv_sem=psem.at[3 + i], device_id=target, device_id_type=MESH,
        )
        for i, target in ((1, sibling), (2, x_near), (3, x_sibling), (4, y_near))
    ]
    for copy in p_copies:
        copy.start()
    mine = [total(2 * d) for d in range(LAYERS)]
    for copy in p_copies:
        copy.wait()
    sums = ps[0] + got[0] + got[1] + got[2] + got[3]
    for d in range(LAYERS):
        live = buf[5 * d + OWN, rows:rows + 16, :].astype(jnp.float32)[0:1, :]
        weight = live / (mine[d] + sums[d:d + 1, :] + 1.0 - live)
        for j in range(owners):
            ws[j, pl.ds(layer[d], 1), 0:slots] = weight[:, j * slots:(j + 1) * slots]

    spot = 2 * gen + y

    def w_copy(j):
        return pltpu.make_async_remote_copy(
            src_ref=ws.at[j], dst_ref=wr.at[spot], send_sem=wsend.at[j],
            recv_sem=wrecv.at[spot], device_id=(z, j), device_id_type=MESH,
        )

    def w_got(i):
        return pltpu.make_async_remote_copy(
            src_ref=ws.at[0], dst_ref=wr.at[i], send_sem=wsend.at[0],
            recv_sem=wrecv.at[i], device_id=y_near, device_id_type=MESH,
        )

    def send(j, carry):
        @pl.when(z * joins + j != me)
        def _():
            w_copy(j).start()

        @pl.when(z * joins + j == me)
        def _():
            wr[spot] = ws[j]

        return carry

    lax.fori_loop(0, owners, send, 0)

    def receive(i, carry):
        @pl.when((i // 2) * joins + 2 * gen + i % 2 != me)
        def _():
            w_got(i).wait_recv()

        return carry

    lax.fori_loop(0, owners, receive, 0)
    out[...] = wr[...]

    def sent(j, carry):
        @pl.when(z * joins + j != me)
        def _():
            w_copy(j).wait_send()

        return carry

    lax.fori_loop(0, owners, sent, 0)
    for d in range(1, LAYERS):
        z_copy(d).wait_send()
    for d in range(LAYERS):
        for kind in (SIB, XN, YN, XS):
            l_copy(d, kind).wait_send()


def layer_body(src_emb, counts):
    block, width = src_emb.shape
    rows = block // LAYERS
    owners = 8
    slots = rows // owners
    slot = lax.broadcasted_iota(jnp.int32, (LAYERS, 16, owners, slots), 3)
    flags = (slot < counts.reshape(LAYERS, 1, owners, 1)).astype(jnp.bfloat16)
    flags = flags.reshape(LAYERS, 16, rows)
    vmem = pl.BlockSpec(memory_space=pltpu.VMEM)
    weights = pl.pallas_call(
        lambda *refs: layer_kernel(rows, width, *refs),
        out_shape=jax.ShapeDtypeStruct((owners, 8, 128), jnp.float32),
        in_specs=[vmem, vmem],
        out_specs=vmem,
        scratch_shapes=[
            pltpu.VMEM((5 * LAYERS, rows + 16, width), jnp.bfloat16),
            pltpu.VMEM((LAYERS - 1, rows + 16, width), jnp.bfloat16),
            pltpu.VMEM((4, rows, 128), jnp.float32),
            pltpu.VMEM((2 * LAYERS, owners, rows), jnp.float32),
            pltpu.VMEM((2 * LAYERS, 8, rows), jnp.float32),
            pltpu.VMEM((4, rows, 128), jnp.float32),
            pltpu.VMEM((5, 8, rows), jnp.float32),
            pltpu.VMEM((4, 8, rows), jnp.float32),
            pltpu.VMEM((owners, 8, 128), jnp.float32),
            pltpu.VMEM((owners, 8, 128), jnp.float32),
            pltpu.SemaphoreType.DMA((LAYERS - 1,)),
            pltpu.SemaphoreType.DMA((LAYERS - 1,)),
            pltpu.SemaphoreType.DMA((4 * LAYERS,)),
            pltpu.SemaphoreType.DMA((4 * LAYERS,)),
            pltpu.SemaphoreType.DMA((8,)),
            pltpu.SemaphoreType.DMA((owners,)),
            pltpu.SemaphoreType.DMA((owners,)),
        ],
        compiler_params=pltpu.CompilerParams(
            collective_id=0, has_side_effects=True, vmem_limit_bytes=56 * 2**20
        ),
        name="layer_kernel",
    )(src_emb, flags)
    weights = weights[:, :LAYERS, :slots].reshape(4, 2, LAYERS, slots)
    return weights.transpose(0, 2, 1, 3).reshape(block)


def solution(mesh):
    in_specs = (P(("gen", "join"), None), P(("gen", "join"), None))
    out_specs = P(("gen", "join"))
    fits = mesh.shape["gen"] == 4 and mesh.shape["join"] == 8
    body = layer_body if fits else ring_body
    return jax.shard_map(body, mesh=mesh, in_specs=in_specs, out_specs=out_specs, check_vma=False)
```

```python
import math

import jax
import jax.numpy as jnp
from jax import lax
from jax.experimental import pallas as pl
from jax.experimental.pallas import tpu as pltpu
from jax.sharding import PartitionSpec as P

ROUNDS = 3
MESH = pl.DeviceIdType.MESH
SCALE = 8.0 * math.log2(math.e)
DEAD = -1e30
LAYERS = 4
OWN, YN, SIB, XN, XS = range(5)


def shifted(block, axis, distance):
    devices = range(lax.axis_size(axis))
    route = [((i - distance) % len(devices), i) for i in devices]
    return lax.ppermute(block, axis, route)


def tile_sums(left_rows, left_live, right_rows, right_live):
    row_count = left_rows.shape[0]
    piece_rows = min(512, row_count)
    pieces = row_count // piece_rows

    def one_piece(col_total, operands):
        piece_block, piece_live = operands
        scores = lax.dot_general(
            piece_block, right_rows, (((1,), (1,)), ((), ())), preferred_element_type=jnp.float32
        )
        kernel = jnp.exp(8.0 * (scores - 1.0))
        return (
            col_total + jnp.sum(kernel * piece_live[:, None], axis=0),
            jnp.sum(kernel * right_live[None, :], axis=1),
        )

    start_total = jnp.zeros((right_rows.shape[0],), jnp.float32)
    col_sums, row_sums = lax.scan(
        one_piece,
        start_total,
        (
            left_rows.reshape(pieces, piece_rows, left_rows.shape[1]),
            left_live.reshape(pieces, piece_rows),
        ),
    )
    return (row_sums.reshape(row_count), col_sums)


def ring_body(src_emb, counts):
    values = src_emb.astype(jnp.float32)
    width = values.shape[1]
    unit = (
        values
        * lax.rsqrt(jnp.mean(values * values, axis=1, keepdims=True) + 1e-06)
        / math.sqrt(width)
    ).astype(jnp.bfloat16)
    nodes = lax.axis_size(("gen", "join"))
    block_rows = unit.shape[0]
    slots = block_rows // nodes
    received, got_counts = (
        lax.all_to_all(
            unit.reshape(nodes, slots, width),
            ("gen", "join"),
            split_axis=0,
            concat_axis=0,
            tiled=True,
        ),
        lax.all_to_all(
            counts.reshape(nodes), ("gen", "join"), split_axis=0, concat_axis=0, tiled=True
        ),
    )
    owned = received.reshape(block_rows, width)
    slot_index = lax.broadcasted_iota(jnp.int32, (nodes, slots), 1)
    live = (slot_index < got_counts.reshape(nodes, 1)).astype(jnp.float32).reshape(block_rows)
    live_wire = live.astype(jnp.bfloat16)
    density = tile_sums(owned, live, owned, live)[0]
    for shift_by in range(1, ROUNDS + 1):
        other_rows, other_flags = shifted((owned, live_wire), "join", shift_by)
        row_sums, col_sums = tile_sums(owned, live, other_rows, other_flags.astype(jnp.float32))
        density = density + row_sums + shifted(col_sums, "join", -shift_by)
    return live / (density + 1.0 - live)


def layer_kernel(rows, width, src, flags, out, buf, snd, bias, mask, acc, cacc, ps, got, ws, wr,
                 zsend, zrecv, lsend, lrecv, psem, wsend, wrecv):
    gen, join = lax.axis_index("gen"), lax.axis_index("join")
    x, k, z, y = gen // 2, gen % 2, join // 2, join % 2
    zh, zl = z // 2, z % 2
    layer = [z, 2 * zh + 1 - zl, 2 * (1 - zh) + zl, 3 - z]
    nodes, joins = 32, 8
    me = gen * joins + join
    sibling = (2 * x + 1 - k, join)
    x_near = (2 * (1 - x) + k, join)
    y_near = (gen, 2 * z + 1 - y)
    owners = 8
    slots = rows // owners

    barrier = pltpu.get_barrier_semaphore()

    def greet(i, carry):
        t = (me + i) % nodes
        pl.semaphore_signal(barrier, inc=1, device_id=(t // joins, t % joins), device_id_type=MESH)
        return carry

    lax.fori_loop(1, nodes, greet, 0)

    def normalize(d, into):
        start = pl.multiple_of(layer[d] * rows, rows)
        values = src[pl.ds(start, rows), :].astype(jnp.float32)
        into[0:rows, :] = (
            values
            * lax.rsqrt(jnp.mean(values * values, axis=1, keepdims=True) + 1e-06)
            / math.sqrt(width)
        ).astype(jnp.bfloat16)
        into[rows:rows + 16, :] = flags[layer[d]]

    halves = (pl.ds(0, rows // 2), pl.ds(rows // 2, rows // 2 + 16))

    def z_copy(d, h):
        return pltpu.make_async_remote_copy(
            src_ref=snd.at[d - 1, halves[h]], dst_ref=buf.at[5 * d + OWN, halves[h]],
            send_sem=zsend.at[2 * d - 2 + h], recv_sem=zrecv.at[2 * d - 2 + h],
            device_id=(gen, 2 * layer[d] + y), device_id_type=MESH,
        )

    def l_copy(d, kind, h):
        source = XN if kind == XS else OWN
        target = {SIB: sibling, XS: sibling, XN: x_near, YN: y_near}[kind]
        sem = 2 * (4 * d + kind - 1) + h
        return pltpu.make_async_remote_copy(
            src_ref=buf.at[5 * d + source, halves[h]], dst_ref=buf.at[5 * d + kind, halves[h]],
            send_sem=lsend.at[sem], recv_sem=lrecv.at[sem],
            device_id=target, device_id_type=MESH,
        )

    def z_start(d):
        for h in range(2):
            z_copy(d, h).start()

    def l_start(d, h):
        for kind in (XN, YN, SIB):
            l_copy(d, kind, h).start()

    def l_wait(d, kind):
        for h in range(2):
            l_copy(d, kind, h).wait_recv()

    lane_owner = lax.broadcasted_iota(jnp.int32, (owners, rows), 1) // slots
    other_owner = (lax.broadcasted_iota(jnp.int32, (owners, rows), 0) + 4) % owners
    near = (other_owner != lane_owner).astype(jnp.float32)

    def at(kind):
        return max(kind - 1, 0)

    def set_bias(d, kind):
        ones = jnp.full((16, 128), 1.0 / 16.0, jnp.bfloat16)
        live = lax.dot_general(
            buf[5 * d + kind, rows:rows + 16, :], ones, (((0,), (0,)), ((), ())),
            preferred_element_type=jnp.float32,
        )
        bias[at(kind)] = jnp.where(live > 0.5, -SCALE, DEAD)

    def set_mask(d, kind):
        live = buf[5 * d + kind, rows:rows + 16, :].astype(jnp.float32)[0:owners, :]
        mask[2 * d + kind] = live * near

    piece = 256

    def tile(row, slot, col, col_slot, both):
        held = buf[row, 0:rows, :]
        for b in range(rows // piece):
            scores = lax.dot_general(
                buf[col, b * piece:(b + 1) * piece, :], held, (((1,), (1,)), ((), ())),
                preferred_element_type=jnp.float32,
            )
            shift = bias[col_slot, b * piece:(b + 1) * piece, :]
            kernel = jnp.exp2(scores * SCALE + jnp.concatenate([shift] * (rows // 128), axis=1))
            count = piece // slots
            kept = mask[slot, count * b:count * (b + 1), :]
            kernel = (kernel.reshape(count, slots, rows) * kept[:, None, :]).reshape(piece, rows)
            acc[slot] += jnp.sum(kernel.reshape(piece // 8, 8, rows), axis=0)
            if both:
                sums = kernel[:, 0:128]
                for t in range(1, rows // 128):
                    sums = sums + kernel[:, 128 * t:128 * (t + 1)]
                cacc[col_slot, b * piece:(b + 1) * piece, :] += sums

    def old_rows(d, kind):
        def step(i, carry):
            for own_or_yn in range(2):
                tile(5 * i + own_or_yn, 2 * i + own_or_yn, 5 * d + kind, at(kind), True)
            return carry

        lax.fori_loop(0, d, step, 0)

    normalize(2, snd.at[1])
    normalize(0, buf.at[OWN])
    pl.semaphore_wait(barrier, nodes - 1)
    z_start(2)
    l_start(0, 0)
    l_start(0, 1)
    normalize(1, snd.at[0])
    z_start(1)
    normalize(3, snd.at[2])
    z_start(3)
    acc[...] = jnp.zeros_like(acc)
    ps[...] = jnp.zeros_like(ps)
    ws[...] = jnp.zeros_like(ws)

    def z_wait(d, h):
        pltpu.make_async_remote_copy(
            src_ref=snd.at[d - 1, halves[h]], dst_ref=buf.at[5 * d + OWN, halves[h]],
            send_sem=zsend.at[2 * d - 2 + h], recv_sem=zrecv.at[2 * d - 2 + h],
            device_id=y_near, device_id_type=MESH,
        ).wait_recv()

    def phase(d, carry):
        cacc[...] = jnp.zeros_like(cacc)
        set_bias(d, OWN)
        set_mask(d, OWN)
        tile(5 * d + OWN, 2 * d, 5 * d + OWN, at(OWN), False)
        old_rows(d, OWN)
        l_wait(d, SIB)
        set_bias(d, SIB)
        tile(5 * d + OWN, 2 * d, 5 * d + SIB, at(SIB), False)
        old_rows(d, SIB)
        for h in range(2):
            l_copy(d, XN, h).wait_recv()
            l_copy(d, XS, h).start()

        @pl.when(d < LAYERS - 2)
        def _():
            for h in range(2):
                z_wait(d + 1, h)
                l_start(d + 1, h)

        set_bias(d, XN)
        tile(5 * d + OWN, 2 * d, 5 * d + XN, at(XN), False)
        old_rows(d, XN)
        l_wait(d, YN)
        set_mask(d, YN)

        def new_row(kk, inner):
            tile(5 * d + YN, 2 * d + 1, 5 * d + kk + (kk + 3) // 4, kk, False)
            return inner

        lax.fori_loop(0, 3, new_row, 0)
        @pl.when(d == LAYERS - 2)
        def _():
            for h in range(2):
                z_wait(d + 1, h)
                l_start(d + 1, h)

        l_wait(d, XS)
        set_bias(d, XS)
        old_rows(d, XS)

        for kind in (OWN, YN):
            tile(5 * d + kind, 2 * d + kind, 5 * d + XS, at(XS), False)

        ones = jnp.ones((8, 128), jnp.float32)
        for slot in range(4):
            sums = lax.dot_general(
                ones, cacc[slot], (((1,), (1,)), ((), ())),
                preferred_element_type=jnp.float32, precision=lax.Precision.HIGHEST,
            )
            ps[slot, pl.ds(d, 1), :] = sums[0:1, :]
        return carry

    lax.fori_loop(0, LAYERS, phase, 0)

    def total(i):
        return jnp.sum(acc[i], axis=0, keepdims=True)

    for d in range(LAYERS):
        ps[4, d:d + 1, :] = total(2 * d + 1)
    x_sibling = (2 * (1 - x) + 1 - k, join)
    p_copies = [
        pltpu.make_async_remote_copy(
            src_ref=ps.at[i], dst_ref=got.at[i - 1], send_sem=psem.at[i - 1],
            recv_sem=psem.at[3 + i], device_id=target, device_id_type=MESH,
        )
        for i, target in ((1, sibling), (2, x_near), (3, x_sibling), (4, y_near))
    ]
    for copy in p_copies:
        copy.start()
    mine = [total(2 * d) for d in range(LAYERS)]
    for copy in p_copies:
        copy.wait()
    sums = ps[0] + got[0] + got[1] + got[2] + got[3]
    for d in range(LAYERS):
        live = buf[5 * d + OWN, rows:rows + 16, :].astype(jnp.float32)[0:1, :]
        weight = live / (mine[d] + sums[d:d + 1, :] + 1.0 - live)
        for j in range(owners):
            ws[j, pl.ds(layer[d], 1), 0:slots] = weight[:, j * slots:(j + 1) * slots]

    spot = 2 * gen + y

    def w_copy(j):
        return pltpu.make_async_remote_copy(
            src_ref=ws.at[j], dst_ref=wr.at[spot], send_sem=wsend.at[j],
            recv_sem=wrecv.at[spot], device_id=(z, j), device_id_type=MESH,
        )

    def w_got(i):
        return pltpu.make_async_remote_copy(
            src_ref=ws.at[0], dst_ref=wr.at[i], send_sem=wsend.at[0],
            recv_sem=wrecv.at[i], device_id=y_near, device_id_type=MESH,
        )

    def send(j, carry):
        @pl.when(z * joins + j != me)
        def _():
            w_copy(j).start()

        @pl.when(z * joins + j == me)
        def _():
            wr[spot] = ws[j]

        return carry

    lax.fori_loop(0, owners, send, 0)

    def receive(i, carry):
        @pl.when((i // 2) * joins + 2 * gen + i % 2 != me)
        def _():
            w_got(i).wait_recv()

        return carry

    lax.fori_loop(0, owners, receive, 0)
    out[...] = wr[...]

    def sent(j, carry):
        @pl.when(z * joins + j != me)
        def _():
            w_copy(j).wait_send()

        return carry

    lax.fori_loop(0, owners, sent, 0)
    for d in range(1, LAYERS):
        for h in range(2):
            z_copy(d, h).wait_send()
    for d in range(LAYERS):
        for kind in (SIB, XN, YN, XS):
            for h in range(2):
                l_copy(d, kind, h).wait_send()


def layer_body(src_emb, counts):
    block, width = src_emb.shape
    rows = block // LAYERS
    owners = 8
    slots = rows // owners
    slot = lax.broadcasted_iota(jnp.int32, (LAYERS, 16, owners, slots), 3)
    flags = (slot < counts.reshape(LAYERS, 1, owners, 1)).astype(jnp.bfloat16)
    flags = flags.reshape(LAYERS, 16, rows)
    vmem = pl.BlockSpec(memory_space=pltpu.VMEM)
    weights = pl.pallas_call(
        lambda *refs: layer_kernel(rows, width, *refs),
        out_shape=jax.ShapeDtypeStruct((owners, 8, 128), jnp.float32),
        in_specs=[vmem, vmem],
        out_specs=vmem,
        scratch_shapes=[
            pltpu.VMEM((5 * LAYERS, rows + 16, width), jnp.bfloat16),
            pltpu.VMEM((LAYERS - 1, rows + 16, width), jnp.bfloat16),
            pltpu.VMEM((4, rows, 128), jnp.float32),
            pltpu.VMEM((2 * LAYERS, owners, rows), jnp.float32),
            pltpu.VMEM((2 * LAYERS, 8, rows), jnp.float32),
            pltpu.VMEM((4, rows, 128), jnp.float32),
            pltpu.VMEM((5, 8, rows), jnp.float32),
            pltpu.VMEM((4, 8, rows), jnp.float32),
            pltpu.VMEM((owners, 8, 128), jnp.float32),
            pltpu.VMEM((owners, 8, 128), jnp.float32),
            pltpu.SemaphoreType.DMA((2 * LAYERS - 2,)),
            pltpu.SemaphoreType.DMA((2 * LAYERS - 2,)),
            pltpu.SemaphoreType.DMA((8 * LAYERS,)),
            pltpu.SemaphoreType.DMA((8 * LAYERS,)),
            pltpu.SemaphoreType.DMA((8,)),
            pltpu.SemaphoreType.DMA((owners,)),
            pltpu.SemaphoreType.DMA((owners,)),
        ],
        compiler_params=pltpu.CompilerParams(
            collective_id=0, has_side_effects=True, vmem_limit_bytes=56 * 2**20
        ),
        name="layer_kernel",
    )(src_emb, flags)
    weights = weights[:, :LAYERS, :slots].reshape(4, 2, LAYERS, slots)
    return weights.transpose(0, 2, 1, 3).reshape(block)


def solution(mesh):
    in_specs = (P(("gen", "join"), None), P(("gen", "join"), None))
    out_specs = P(("gen", "join"))
    fits = mesh.shape["gen"] == 4 and mesh.shape["join"] == 8
    body = layer_body if fits else ring_body
    return jax.shard_map(body, mesh=mesh, in_specs=in_specs, out_specs=out_specs, check_vma=False)
```
